32 devices in a mesh: seq: 8 (over z, y), head: 4 (over x, core).
Axes of the slice: x: 2, y: 2, z: 4, core: 2. Of those that a mesh axis runs over, the one named last changes fastest.
Arguments:
- query: bfloat16 [4096, 1024], P('seq', 'head'), may hold values from -70 to 70
- key: bfloat16 [4096, 1024], P('seq', 'head'), may hold values from -15 to 15
- value: bfloat16 [4096, 1024], P('seq', 'head'), may hold values from -6 to 6
- middle_offsets: int32 [16], P('head'), may hold values from 0 to 3
- upper_offsets: int32 [16], P('head'), may hold values from 0 to 3
- out_weight: bfloat16 [1024, 1024], P('head'), may hold values from -0.1875 to 0.1875
Outputs:
- projected: bfloat16 [4096, 1024], P(('seq', 'head'))
The draws below stay inside these ranges and needn't reach their ends.
All inputs are finite; a program needn't handle non-finite values.
Results may differ from the reference program's by a relative error of at most 0.0051.
Values may be sent and summed in bfloat16 or wider, within the bound.
A program may use at most 64 MiB of HBM per device.

```python
import jax
import jax.numpy as jnp
from jax import lax

D = 1024
HEAD_TOTAL = 16
HD = 64
TOKENS_PER_SHARD = 512
SPAN = 8
MIDDLE_DILATION = 4
TOP_DILATION = 4
TOKENS = 4096
N_SEQ = 8


def draw_query(key, part):
    normal_part = jnp.clip(jax.random.normal(jax.random.fold_in(key, 1), (TOKENS, HEAD_TOTAL * HD), jnp.float32), -6.0, 6.0)
    return normal_part.astype(jnp.bfloat16)


def draw_key(key, part):
    normal_part = jnp.clip(jax.random.normal(jax.random.fold_in(key, 3), (TOKENS, HEAD_TOTAL * HD), jnp.float32), -6.0, 6.0)
    return (normal_part * 2.5).astype(jnp.bfloat16)


def touch_ends(drawn, own_key, smallest, largest):
    longest = drawn.shape.index(max(drawn.shape))
    spots = []
    for shift in (0, 1):
        where = [jax.random.randint(jax.random.fold_in(own_key, axis), (), 0, length) for axis, length in enumerate(drawn.shape)]
        where[longest] = (where[longest] + shift) % drawn.shape[longest]
        spots.append(tuple(where))
    return drawn.at[spots[0]].set(smallest).at[spots[1]].set(largest)


def steps_of(own_key, extent, shards, low, largest):
    def one(position, blocks):
        draws = jax.random.uniform(jax.random.fold_in(jax.random.fold_in(own_key, 6), position), (blocks,), jnp.float32, low / len(shards), largest / len(shards))
        return jnp.repeat(jnp.exp(draws), extent[position] // blocks).reshape((-1,) + (1,) * (len(extent) - position - 1))

    loudness = one(*shards[0])
    for cut in shards[1:]:
        loudness = loudness * one(*cut)
    return loudness


def bell_draw(stream_key, extent, width, bound, cuts=(), held_as=jnp.bfloat16):
    values = jax.random.normal(stream_key, extent, jnp.float32) * width
    if len(cuts) > 0:
        values = steps_of(stream_key, extent, cuts, -0.22, 0.18) * values
    return jnp.clip(values, min=-bound, max=bound).astype(held_as)


def setup_inputs(seed: int = 0) -> dict:
    key_of = jax.random.split(jax.random.key(seed), 7)
    query = draw_query(jax.random.fold_in(key_of[6], 71), 0)
    key = draw_key(jax.random.fold_in(key_of[6], 71), 0)
    value = bell_draw(key_of[2], (TOKENS, HEAD_TOTAL * HD), 1.0, 6.0, ((0, 8), (1, 4)))
    middle_offsets = touch_ends(jax.random.randint(key_of[3], (HEAD_TOTAL,), 0, MIDDLE_DILATION), jax.random.fold_in(key_of[3], 1), 0, MIDDLE_DILATION - 1).astype(jnp.int32)
    upper_offsets = touch_ends(jax.random.randint(key_of[4], (HEAD_TOTAL,), 0, TOP_DILATION), jax.random.fold_in(key_of[4], 1), 0, TOP_DILATION - 1).astype(jnp.int32)
    out_weight = bell_draw(key_of[5], (HEAD_TOTAL * HD, D), (HEAD_TOTAL * HD) ** -0.5, 0.1875, ((0, 4),))
    return {"query": query, "key": key, "value": value, "middle_offsets": middle_offsets, "upper_offsets": upper_offsets, "out_weight": out_weight}


def attend_segment(query_matrix_rows, key_matrix_rows, value_matrix_rows):
    scores = jnp.einsum("qhd,khd->hqk", query_matrix_rows.astype(jnp.float32), key_matrix_rows.astype(jnp.float32)) * (HD ** -0.5)
    row_max = jnp.max(scores, axis=2)
    mass = jnp.exp(scores - row_max[:, :, None])
    total = jnp.sum(mass, axis=2)
    soft_weights = mass.astype(jnp.bfloat16)
    weighted = jnp.einsum("hqk,khd->qhd", soft_weights.astype(jnp.float32), value_matrix_rows.astype(jnp.float32))
    return weighted, total.T, row_max.T


def attend_trio(trio):
    return attend_segment(trio[0], trio[1], trio[2])


def picked_rows(block_rows, offsets, stride):
    group_count = block_rows.shape[0] // stride
    grouped = block_rows.reshape(group_count, stride, block_rows.shape[1], block_rows.shape[2])
    gather_index = jnp.broadcast_to(offsets.astype(jnp.int32)[None, None, :, None], (group_count, 1, block_rows.shape[1], block_rows.shape[2]))
    return jnp.take_along_axis(grouped, gather_index, axis=1)[:, 0]


def scatter_rows(values, offsets, stride, filler):
    chosen = jnp.arange(stride, dtype=jnp.int32)[:, None] == offsets.astype(jnp.int32)[None, :]
    chosen = chosen.reshape(chosen.shape + (1,) * (values.ndim - 2))
    spread_out = jnp.where(chosen[None], values[:, None], filler)
    return spread_out.reshape((values.shape[0] * stride,) + values.shape[1:])


def combine(levels):
    highest = levels[0][2]
    for one_level in levels[1:]:
        highest = jnp.maximum(highest, one_level[2])
    numerator = jnp.zeros(levels[0][0].shape, jnp.float32)
    denominator = jnp.zeros(levels[0][1].shape, jnp.float32)
    for one_level in levels:
        factor = jnp.exp(one_level[2] - highest)
        numerator = numerator + factor[:, :, None] * one_level[0]
        denominator = denominator + factor * one_level[1]
    return (numerator / denominator[:, :, None]).astype(jnp.bfloat16)


def reference(query, key, value, middle_offsets, upper_offsets, out_weight):
    query_matrix_rows = query.reshape(TOKENS, HEAD_TOTAL, HD)
    key_matrix_rows = key.reshape(TOKENS, HEAD_TOTAL, HD)
    value_matrix_rows = value.reshape(TOKENS, HEAD_TOTAL, HD)
    upper_result = attend_segment(picked_rows(query_matrix_rows, upper_offsets, TOP_DILATION), picked_rows(key_matrix_rows, upper_offsets, TOP_DILATION), picked_rows(value_matrix_rows, upper_offsets, TOP_DILATION))
    segment_length = SPAN * TOKENS_PER_SHARD
    upper_per_segment = segment_length // TOP_DILATION

    def one_segment(segment):
        row_begin = segment * segment_length
        segment_query = lax.dynamic_slice_in_dim(query_matrix_rows, row_begin, segment_length, 0)
        segment_key = lax.dynamic_slice_in_dim(key_matrix_rows, row_begin, segment_length, 0)
        segment_value = lax.dynamic_slice_in_dim(value_matrix_rows, row_begin, segment_length, 0)
        bottom = lax.map(attend_trio, (segment_query.reshape(SPAN, TOKENS_PER_SHARD, HEAD_TOTAL, HD), segment_key.reshape(SPAN, TOKENS_PER_SHARD, HEAD_TOTAL, HD), segment_value.reshape(SPAN, TOKENS_PER_SHARD, HEAD_TOTAL, HD)))
        bottom = (bottom[0].reshape(segment_length, HEAD_TOTAL, HD), bottom[1].reshape(segment_length, HEAD_TOTAL), bottom[2].reshape(segment_length, HEAD_TOTAL))
        middle_level = attend_segment(picked_rows(segment_query, middle_offsets, MIDDLE_DILATION), picked_rows(segment_key, middle_offsets, MIDDLE_DILATION), picked_rows(segment_value, middle_offsets, MIDDLE_DILATION))
        middle_level = (scatter_rows(middle_level[0], middle_offsets, MIDDLE_DILATION, 0.0), scatter_rows(middle_level[1], middle_offsets, MIDDLE_DILATION, 0.0), scatter_rows(middle_level[2], middle_offsets, MIDDLE_DILATION, -jnp.inf))
        top_start = segment * upper_per_segment
        upper_level = tuple(lax.dynamic_slice_in_dim(member, top_start, upper_per_segment, 0) for member in upper_result)
        upper_level = (scatter_rows(upper_level[0], upper_offsets, TOP_DILATION, 0.0), scatter_rows(upper_level[1], upper_offsets, TOP_DILATION, 0.0), scatter_rows(upper_level[2], upper_offsets, TOP_DILATION, -jnp.inf))
        attention = combine((bottom, middle_level, upper_level)).reshape(segment_length, HEAD_TOTAL * HD)
        return jnp.dot(attention, out_weight, preferred_element_type=jnp.float32).astype(jnp.bfloat16)

    outputs = lax.map(one_segment, jnp.arange(N_SEQ // SPAN, dtype=jnp.int32))
    return outputs.reshape(TOKENS, D)
```

```python
import functools

import jax
import jax.numpy as jnp
from jax import lax
from jax.experimental import pallas as pl
from jax.experimental.pallas import tpu as pltpu
from jax.sharding import PartitionSpec as P

HD = 64
SPAN = 8
MIDDLE_DILATION = 4


def partner_2(value, axis, stride):
    mask = 2**stride
    pairs = [(source, source ^ mask) for source in range(lax.axis_size(axis))]
    return lax.ppermute(value, axis, pairs)


def attend_segment(query_matrix_rows, key_matrix_rows, value_matrix_rows):
    scores = jnp.einsum(
        "qhd,khd->hqk", query_matrix_rows, key_matrix_rows, preferred_element_type=jnp.float32
    ) * HD ** (-0.5)
    row_max = jnp.max(scores, axis=2)
    mass = jnp.exp(scores - row_max[:, :, None])
    total = jnp.sum(mass, axis=2)
    soft_weights = mass.astype(jnp.bfloat16)
    weighted = jnp.einsum(
        "hqk,khd->qhd", soft_weights, value_matrix_rows, preferred_element_type=jnp.float32
    )
    return (weighted, total.T, row_max.T)


def attend_blocks(query_matrix_rows, key_matrix_rows, value_matrix_rows):
    block_size = min(512, query_matrix_rows.shape[0])
    pieces = query_matrix_rows.reshape(
        query_matrix_rows.shape[0] // block_size,
        block_size,
        query_matrix_rows.shape[1],
        query_matrix_rows.shape[2],
    )

    def one_block(one_piece):
        return attend_segment(one_piece, key_matrix_rows, value_matrix_rows)

    weighted, total, row_max = lax.map(one_block, pieces)
    return (
        weighted.reshape(query_matrix_rows.shape),
        total.reshape(query_matrix_rows.shape[:2]),
        row_max.reshape(query_matrix_rows.shape[:2]),
    )


def picked_rows(block_rows, offsets, stride):
    group_count = block_rows.shape[0] // stride
    grouped = block_rows.reshape(group_count, stride, block_rows.shape[1], block_rows.shape[2])
    chosen = (
        jnp.arange(stride, dtype=jnp.int32)[None, :, None, None] == offsets[None, None, :, None]
    )
    return jnp.sum(jnp.where(chosen, grouped, jnp.zeros((), grouped.dtype)), axis=1)


def scatter_rows(values, offsets, stride, filler):
    chosen = jnp.arange(stride, dtype=jnp.int32)[:, None] == offsets[None, :]
    spread_out = jnp.where(chosen[None], values[:, None], filler)
    return spread_out.reshape((values.shape[0] * stride,) + values.shape[1:])


def flatten_level(result):
    row_total = result[0].shape[0]
    weighted = result[0].reshape(row_total, -1)
    total = jnp.repeat(result[1], HD, axis=1)
    row_max = jnp.repeat(result[2], HD, axis=1)
    return (weighted, total, row_max)


def scatter_level(result, offsets, stride):
    weighted, total, row_max = flatten_level(result)
    column_offsets = jnp.repeat(offsets, HD)
    return (
        scatter_rows(weighted, column_offsets, stride, 0.0),
        scatter_rows(total, column_offsets, stride, 0.0),
        scatter_rows(row_max, column_offsets, stride, -jnp.inf),
    )


def combine(levels):
    highest = levels[0][2]
    for one_level in levels[1:]:
        highest = jnp.maximum(highest, one_level[2])
    numerator = jnp.zeros(levels[0][0].shape, jnp.float32)
    denominator = jnp.zeros(levels[0][1].shape, jnp.float32)
    for one_level in levels:
        factor = jnp.exp(one_level[2] - highest)
        numerator = numerator + factor * one_level[0]
        denominator = denominator + factor * one_level[1]
    return (numerator / denominator).astype(jnp.bfloat16)


def per_device(query, key, value, middle_offsets, upper_offsets, out_weight):
    row_count = query.shape[0]
    head_count = query.shape[1] // HD
    top_stride = lax.axis_size("seq") // 2
    query_matrix_rows = query.reshape(row_count, head_count, HD)
    key_matrix_rows = key.reshape(row_count, head_count, HD)
    value_matrix_rows = value.reshape(row_count, head_count, HD)
    top_key_local = picked_rows(key_matrix_rows, upper_offsets, top_stride).reshape(
        -1, head_count * HD
    )
    top_value_local = picked_rows(value_matrix_rows, upper_offsets, top_stride).reshape(
        -1, head_count * HD
    )
    top_key_all, top_value_all = (
        lax.all_gather(top_key_local, "seq", axis=0, tiled=True),
        lax.all_gather(top_value_local, "seq", axis=0, tiled=True),
    )
    upper_level = attend_segment(
        picked_rows(query_matrix_rows, upper_offsets, top_stride),
        top_key_all.reshape(-1, head_count, HD),
        top_value_all.reshape(-1, head_count, HD),
    )
    middle_pair = jnp.stack(
        [
            picked_rows(key_matrix_rows, middle_offsets, MIDDLE_DILATION),
            picked_rows(value_matrix_rows, middle_offsets, MIDDLE_DILATION),
        ]
    ).reshape(2, -1, head_count * HD)
    for bit_number in range(SPAN.bit_length() - 1):
        partner = partner_2(middle_pair, "seq", bit_number)
        middle_pair = jnp.concatenate([middle_pair, partner], axis=1)
    middle_level = attend_segment(
        picked_rows(query_matrix_rows, middle_offsets, MIDDLE_DILATION),
        middle_pair[0].reshape(-1, head_count, HD),
        middle_pair[1].reshape(-1, head_count, HD),
    )
    bottom = flatten_level(attend_blocks(query_matrix_rows, key_matrix_rows, value_matrix_rows))
    attention = combine(
        (
            bottom,
            scatter_level(middle_level, middle_offsets, MIDDLE_DILATION),
            scatter_level(upper_level, upper_offsets, top_stride),
        )
    )
    summed = lax.psum_scatter(
        jnp.dot(attention, out_weight, preferred_element_type=jnp.float32),
        "head",
        scatter_dimension=0,
        tiled=True,
    )
    return summed.astype(jnp.bfloat16)


MESH = pl.DeviceIdType.MESH
STAT_ROWS = 16


def dot_f32(left, right):
    return jnp.dot(left, right, preferred_element_type=jnp.float32)


def three_parts(value):
    high = value.astype(jnp.bfloat16).astype(jnp.float32)
    rest = value - high
    middle = rest.astype(jnp.bfloat16).astype(jnp.float32)
    return [high, middle, rest - middle]


def fused_kernel(
    seq_total,
    query_ref,
    key_ref,
    value_ref,
    middle_ref,
    upper_ref,
    weight_ref,
    out_ref,
    select,
    message,
    got,
    result,
    returned,
    bottom,
    bottom_stats,
    columns,
    columns_got,
    weights_got,
    send_pick,
    recv_pick,
    send_back,
    recv_back,
    send_columns,
    recv_columns,
    send_weight,
    recv_weight,
):
    seq, head = lax.axis_index("seq"), lax.axis_index("head")
    chip, core = lax.div(head, 2), lax.rem(head, 2)
    peers = [
        head,
        2 * chip + (1 - core),
        2 * (1 - chip) + core,
        2 * (1 - chip) + (1 - core),
    ]
    rows = query_ref.shape[0]
    heads = query_ref.shape[1] // HD
    taken = rows // MIDDLE_DILATION
    offset_refs = (middle_ref, upper_ref)

    barrier = pltpu.get_barrier_semaphore()
    for step in range(1, seq_total):
        pl.semaphore_signal(
            barrier,
            inc=1,
            device_id=(lax.rem(seq + step, seq_total), head),
            device_id_type=MESH,
        )
    for step in range(1, 4):
        pl.semaphore_signal(
            barrier, inc=1, device_id=(seq, peers[step]), device_id_type=MESH
        )

    query_t = (query_ref[...] * jnp.bfloat16(HD**-0.5)).T
    value_t = value_ref[...].T
    distance = lax.broadcasted_iota(jnp.int32, (taken, rows), 1) - MIDDLE_DILATION * (
        lax.broadcasted_iota(jnp.int32, (taken, rows), 0)
    )
    for level in range(2):
        for one in range(heads):
            pair = level * heads + one
            span = slice(one * HD, (one + 1) * HD)
            chosen = jnp.where(
                distance == offset_refs[level][one], jnp.float32(1), jnp.float32(0)
            ).astype(jnp.bfloat16)
            select[pair] = chosen
            both_t = jnp.concatenate([query_t[span], value_t[span]], axis=0)
            message[pair, 0 : 2 * HD] = lax.dot_general(
                both_t,
                chosen,
                (((1,), (1,)), ((), ())),
                preferred_element_type=jnp.float32,
            ).astype(jnp.bfloat16)
            picked = dot_f32(chosen, key_ref[:, span])
            message[pair, 2 * HD : 3 * HD] = jnp.concatenate(
                [picked[: taken // 2], picked[taken // 2 :]], axis=1
            ).astype(jnp.bfloat16)

    pl.semaphore_wait(barrier, seq_total + 2)
    picks = []
    for step in range(1, seq_total):
        target = lax.rem(seq + step, seq_total)
        picks.append(
            pltpu.make_async_remote_copy(
                src_ref=message.at[target],
                dst_ref=got.at[step],
                send_sem=send_pick.at[step],
                recv_sem=recv_pick.at[step],
                device_id=(target, head),
                device_id_type=MESH,
            )
        )
        picks[-1].start()
    got[0] = message[seq]

    def weight_copy(source, slot, peer):
        return pltpu.make_async_remote_copy(
            src_ref=source,
            dst_ref=weights_got.at[slot],
            send_sem=send_weight.at[slot],
            recv_sem=recv_weight.at[slot],
            device_id=(seq, peers[peer]),
            device_id_type=MESH,
        )

    across = weight_copy(weight_ref, 2, 2)
    across.start()
    beside = weight_copy(weight_ref, 1, 1)
    beside.start()

    half = rows // 2
    for one in range(heads):
        span = slice(one * HD, (one + 1) * HD)
        for part in range(2):
            lanes = slice(part * half, (part + 1) * half)
            scores = dot_f32(key_ref[:, span], query_t[span, lanes])
            row_max = jnp.max(scores, axis=0, keepdims=True)
            mass = jnp.exp(scores - row_max)
            bottom_stats[one, 0:1, lanes] = row_max
            bottom_stats[one, 1:2, lanes] = jnp.sum(mass, axis=0, keepdims=True)
            bottom[one, :, lanes] = dot_f32(value_t[span], mass.astype(jnp.bfloat16))

    for copy in picks:
        copy.wait_recv()
    keys = jnp.concatenate([got[i, 2 * HD : 3 * HD] for i in range(seq_total)], axis=0)
    values_t = jnp.concatenate([got[i, HD : 2 * HD] for i in range(seq_total)], axis=1)
    backs = []
    for part in range(seq_total // 2):
        block = jnp.concatenate(
            [got[2 * part, 0:HD], got[2 * part + 1, 0:HD]], axis=1
        )
        blank = jnp.zeros_like(block)
        first = dot_f32(keys, jnp.concatenate([block, blank], axis=0))
        second = dot_f32(keys, jnp.concatenate([blank, block], axis=0))
        row_max = jnp.maximum(
            jnp.max(first, axis=0, keepdims=True), jnp.max(second, axis=0, keepdims=True)
        )
        first = jnp.exp(first - row_max)
        second = jnp.exp(second - row_max)
        total = jnp.sum(first, axis=0, keepdims=True) + jnp.sum(
            second, axis=0, keepdims=True
        )
        first = first.astype(jnp.bfloat16)
        second = second.astype(jnp.bfloat16)
        pieces = []
        for i in range(seq_total):
            pieces.append(first[i * HD : (i + 1) * HD])
            pieces.append(second[i * HD : (i + 1) * HD])
        weighted = dot_f32(values_t, jnp.concatenate(pieces, axis=0))
        stats = three_parts(row_max) + three_parts(total)
        stats.append(jnp.zeros((STAT_ROWS - len(stats), 2 * taken), jnp.float32))
        packed = jnp.concatenate([weighted] + stats, axis=0).astype(jnp.bfloat16)
        for step in (2 * part, 2 * part + 1):
            begin = (step - 2 * part) * taken
            result[step] = packed[:, begin : begin + taken]
            if step == 0:
                returned[seq] = packed[:, begin : begin + taken]
                continue
            backs.append(
                pltpu.make_async_remote_copy(
                    src_ref=result.at[step],
                    dst_ref=returned.at[seq],
                    send_sem=send_back.at[step],
                    recv_sem=recv_back.at[step],
                    device_id=(lax.rem(seq - step + seq_total, seq_total), head),
                    device_id_type=MESH,
                )
            )
            backs[-1].start()

    across.wait_recv()
    onward = weight_copy(weights_got.at[2], 3, 1)
    onward.start()

    for step in range(1, seq_total):
        pltpu.make_async_remote_copy(
            src_ref=result.at[step],
            dst_ref=returned.at[lax.rem(seq + step, seq_total)],
            send_sem=send_back.at[step],
            recv_sem=recv_back.at[step],
            device_id=(lax.rem(seq + step, seq_total), head),
            device_id_type=MESH,
        ).wait_recv()
    residue = lax.rem(lax.broadcasted_iota(jnp.int32, (1, rows), 1), MIDDLE_DILATION)
    for one in range(heads):
        maxima = [bottom_stats[one, 0:1]]
        totals = [bottom_stats[one, 1:2]]
        sums = [bottom[one]]
        for level in range(2):
            pair = level * heads + one
            spread = dot_f32(returned[pair], select[pair])
            row_max = spread[HD : HD + 1] + spread[HD + 1 : HD + 2] + spread[HD + 2 : HD + 3]
            maxima.append(
                jnp.where(residue == offset_refs[level][one], row_max, -jnp.inf)
            )
            totals.append(
                spread[HD + 3 : HD + 4] + spread[HD + 4 : HD + 5] + spread[HD + 5 : HD + 6]
            )
            sums.append(spread[0:HD])
        highest = jnp.maximum(jnp.maximum(maxima[0], maxima[1]), maxima[2])
        factors = [jnp.exp(row_max - highest) for row_max in maxima]
        denominator = sum(f * t for f, t in zip(factors, totals))
        inverse = 1.0 / denominator
        attention = sum((f * inverse) * w for f, w in zip(factors, sums)).astype(
            jnp.bfloat16
        )
        for i in range(4):
            columns[i, one * HD : (one + 1) * HD] = attention[
                :, i * taken : (i + 1) * taken
            ]

    sent = []
    for step in range(1, 4):
        sent.append(
            pltpu.make_async_remote_copy(
                src_ref=columns.at[peers[step]],
                dst_ref=columns_got.at[step],
                send_sem=send_columns.at[step],
                recv_sem=recv_columns.at[step],
                device_id=(seq, peers[step]),
                device_id_type=MESH,
            )
        )
        sent[-1].start()
    projected = dot_f32(columns[head].T, weight_ref[...])
    for step, weight in ((1, beside), (2, None), (3, onward)):
        if weight is not None:
            weight.wait_recv()
        sent[step - 1].wait_recv()
        projected += dot_f32(columns_got[step].T, weights_got[step])
    out_ref[...] = projected.astype(out_ref.dtype)
    for copy in picks + backs + sent + [across, beside, onward]:
        copy.wait_send()


def per_device_fused(query, key, value, middle_offsets, upper_offsets, out_weight):
    rows, width = query.shape
    seq_total = lax.axis_size("seq")
    heads = width // HD
    pairs = 2 * heads
    taken = rows // MIDDLE_DILATION
    whole = pl.BlockSpec(memory_space=pltpu.VMEM)
    scalars = pl.BlockSpec(memory_space=pltpu.SMEM)
    dma = pltpu.SemaphoreType.DMA
    return pl.pallas_call(
        functools.partial(fused_kernel, seq_total),
        out_shape=jax.ShapeDtypeStruct((rows // 4, out_weight.shape[1]), jnp.bfloat16),
        in_specs=[whole, whole, whole, scalars, scalars, whole],
        out_specs=whole,
        scratch_shapes=[
            pltpu.VMEM((pairs, taken, rows), jnp.bfloat16),
            pltpu.VMEM((pairs, 3 * HD, taken), jnp.bfloat16),
            pltpu.VMEM((seq_total, 3 * HD, taken), jnp.bfloat16),
            pltpu.VMEM((seq_total, HD + STAT_ROWS, taken), jnp.bfloat16),
            pltpu.VMEM((pairs, HD + STAT_ROWS, taken), jnp.bfloat16),
            pltpu.VMEM((heads, HD, rows), jnp.float32),
            pltpu.VMEM((heads, 8, rows), jnp.float32),
            pltpu.VMEM((4, width, taken), jnp.bfloat16),
            pltpu.VMEM((4, width, taken), jnp.bfloat16),
            pltpu.VMEM((4,) + out_weight.shape, jnp.bfloat16),
            dma((seq_total,)),
            dma((seq_total,)),
            dma((seq_total,)),
            dma((seq_total,)),
            dma((4,)),
            dma((4,)),
            dma((4,)),
            dma((4,)),
        ],
        compiler_params=pltpu.CompilerParams(
            collective_id=0, has_side_effects=True, vmem_limit_bytes=48 * 2**20
        ),
    )(query, key, value, middle_offsets, upper_offsets, out_weight)


def solution(mesh):
    in_specs = (
        P("seq", "head"),
        P("seq", "head"),
        P("seq", "head"),
        P("head"),
        P("head"),
        P("head", None),
    )
    out_specs = P(("seq", "head"), None)
    seq_total, head_shards = mesh.shape["seq"], mesh.shape["head"]
    one_segment = seq_total == SPAN and seq_total // 2 == MIDDLE_DILATION and head_shards == 4
    return jax.shard_map(
        per_device_fused if one_segment else per_device, mesh=mesh, in_specs=in_specs, out_specs=out_specs, check_vma=False
    )
```

```python
import functools

import jax
import jax.numpy as jnp
from jax import lax
from jax.experimental import pallas as pl
from jax.experimental.pallas import tpu as pltpu
from jax.sharding import PartitionSpec as P

HD = 64
SPAN = 8
MIDDLE_DILATION = 4


def partner_2(value, axis, stride):
    mask = 2**stride
    pairs = [(source, source ^ mask) for source in range(lax.axis_size(axis))]
    return lax.ppermute(value, axis, pairs)


def attend_segment(query_matrix_rows, key_matrix_rows, value_matrix_rows):
    scores = jnp.einsum(
        "qhd,khd->hqk", query_matrix_rows, key_matrix_rows, preferred_element_type=jnp.float32
    ) * HD ** (-0.5)
    row_max = jnp.max(scores, axis=2)
    mass = jnp.exp(scores - row_max[:, :, None])
    total = jnp.sum(mass, axis=2)
    soft_weights = mass.astype(jnp.bfloat16)
    weighted = jnp.einsum(
        "hqk,khd->qhd", soft_weights, value_matrix_rows, preferred_element_type=jnp.float32
    )
    return (weighted, total.T, row_max.T)


def attend_blocks(query_matrix_rows, key_matrix_rows, value_matrix_rows):
    block_size = min(512, query_matrix_rows.shape[0])
    pieces = query_matrix_rows.reshape(
        query_matrix_rows.shape[0] // block_size,
        block_size,
        query_matrix_rows.shape[1],
        query_matrix_rows.shape[2],
    )

    def one_block(one_piece):
        return attend_segment(one_piece, key_matrix_rows, value_matrix_rows)

    weighted, total, row_max = lax.map(one_block, pieces)
    return (
        weighted.reshape(query_matrix_rows.shape),
        total.reshape(query_matrix_rows.shape[:2]),
        row_max.reshape(query_matrix_rows.shape[:2]),
    )


def picked_rows(block_rows, offsets, stride):
    group_count = block_rows.shape[0] // stride
    grouped = block_rows.reshape(group_count, stride, block_rows.shape[1], block_rows.shape[2])
    chosen = (
        jnp.arange(stride, dtype=jnp.int32)[None, :, None, None] == offsets[None, None, :, None]
    )
    return jnp.sum(jnp.where(chosen, grouped, jnp.zeros((), grouped.dtype)), axis=1)


def scatter_rows(values, offsets, stride, filler):
    chosen = jnp.arange(stride, dtype=jnp.int32)[:, None] == offsets[None, :]
    spread_out = jnp.where(chosen[None], values[:, None], filler)
    return spread_out.reshape((values.shape[0] * stride,) + values.shape[1:])


def flatten_level(result):
    row_total = result[0].shape[0]
    weighted = result[0].reshape(row_total, -1)
    total = jnp.repeat(result[1], HD, axis=1)
    row_max = jnp.repeat(result[2], HD, axis=1)
    return (weighted, total, row_max)


def scatter_level(result, offsets, stride):
    weighted, total, row_max = flatten_level(result)
    column_offsets = jnp.repeat(offsets, HD)
    return (
        scatter_rows(weighted, column_offsets, stride, 0.0),
        scatter_rows(total, column_offsets, stride, 0.0),
        scatter_rows(row_max, column_offsets, stride, -jnp.inf),
    )


def combine(levels):
    highest = levels[0][2]
    for one_level in levels[1:]:
        highest = jnp.maximum(highest, one_level[2])
    numerator = jnp.zeros(levels[0][0].shape, jnp.float32)
    denominator = jnp.zeros(levels[0][1].shape, jnp.float32)
    for one_level in levels:
        factor = jnp.exp(one_level[2] - highest)
        numerator = numerator + factor * one_level[0]
        denominator = denominator + factor * one_level[1]
    return (numerator / denominator).astype(jnp.bfloat16)


def per_device(query, key, value, middle_offsets, upper_offsets, out_weight):
    row_count = query.shape[0]
    head_count = query.shape[1] // HD
    top_stride = lax.axis_size("seq") // 2
    query_matrix_rows = query.reshape(row_count, head_count, HD)
    key_matrix_rows = key.reshape(row_count, head_count, HD)
    value_matrix_rows = value.reshape(row_count, head_count, HD)
    top_key_local = picked_rows(key_matrix_rows, upper_offsets, top_stride).reshape(
        -1, head_count * HD
    )
    top_value_local = picked_rows(value_matrix_rows, upper_offsets, top_stride).reshape(
        -1, head_count * HD
    )
    top_key_all, top_value_all = (
        lax.all_gather(top_key_local, "seq", axis=0, tiled=True),
        lax.all_gather(top_value_local, "seq", axis=0, tiled=True),
    )
    upper_level = attend_segment(
        picked_rows(query_matrix_rows, upper_offsets, top_stride),
        top_key_all.reshape(-1, head_count, HD),
        top_value_all.reshape(-1, head_count, HD),
    )
    middle_pair = jnp.stack(
        [
            picked_rows(key_matrix_rows, middle_offsets, MIDDLE_DILATION),
            picked_rows(value_matrix_rows, middle_offsets, MIDDLE_DILATION),
        ]
    ).reshape(2, -1, head_count * HD)
    for bit_number in range(SPAN.bit_length() - 1):
        partner = partner_2(middle_pair, "seq", bit_number)
        middle_pair = jnp.concatenate([middle_pair, partner], axis=1)
    middle_level = attend_segment(
        picked_rows(query_matrix_rows, middle_offsets, MIDDLE_DILATION),
        middle_pair[0].reshape(-1, head_count, HD),
        middle_pair[1].reshape(-1, head_count, HD),
    )
    bottom = flatten_level(attend_blocks(query_matrix_rows, key_matrix_rows, value_matrix_rows))
    attention = combine(
        (
            bottom,
            scatter_level(middle_level, middle_offsets, MIDDLE_DILATION),
            scatter_level(upper_level, upper_offsets, top_stride),
        )
    )
    summed = lax.psum_scatter(
        jnp.dot(attention, out_weight, preferred_element_type=jnp.float32),
        "head",
        scatter_dimension=0,
        tiled=True,
    )
    return summed.astype(jnp.bfloat16)


MESH = pl.DeviceIdType.MESH
STAT_ROWS = 16


def dot_f32(left, right):
    return jnp.dot(left, right, preferred_element_type=jnp.float32)


def three_parts(value):
    high = value.astype(jnp.bfloat16).astype(jnp.float32)
    rest = value - high
    middle = rest.astype(jnp.bfloat16).astype(jnp.float32)
    return [high, middle, rest - middle]


def fused_kernel(
    seq_total,
    query_hbm,
    key_hbm,
    value_hbm,
    middle_hbm,
    upper_hbm,
    weight_hbm,
    out_ref,
    query_ref,
    key_ref,
    value_ref,
    middle_ref,
    upper_ref,
    weight_ref,
    load,
    select,
    message,
    got,
    result,
    returned,
    bottom,
    bottom_stats,
    columns,
    columns_got,
    weights_got,
    send_pick,
    recv_pick,
    send_back,
    recv_back,
    send_columns,
    recv_columns,
    send_weight,
    recv_weight,
):
    seq, head = lax.axis_index("seq"), lax.axis_index("head")
    chip, core = lax.div(head, 2), lax.rem(head, 2)
    peers = [
        head,
        2 * chip + (1 - core),
        2 * (1 - chip) + core,
        2 * (1 - chip) + (1 - core),
    ]
    rows = query_ref.shape[0]
    heads = query_ref.shape[1] // HD
    half, place = lax.div(seq, heads), lax.rem(seq, heads)
    taken = rows // MIDDLE_DILATION
    offset_refs = (middle_ref, upper_ref)

    loads = []
    for i, (source, target) in enumerate(
        (
            (middle_hbm, middle_ref),
            (upper_hbm, upper_ref),
            (query_hbm, query_ref),
            (value_hbm, value_ref),
            (key_hbm, key_ref),
            (weight_hbm, weight_ref),
        )
    ):
        loads.append(pltpu.make_async_copy(source, target, load.at[i]))
        loads[-1].start()

    barrier = pltpu.get_barrier_semaphore()
    for step in range(1, seq_total):
        pl.semaphore_signal(
            barrier,
            inc=1,
            device_id=(lax.rem(seq + step, seq_total), head),
            device_id_type=MESH,
        )
    for step in range(1, 4):
        pl.semaphore_signal(
            barrier, inc=1, device_id=(seq, peers[step]), device_id_type=MESH
        )

    for copy in loads[:5]:
        copy.wait()
    query_t = (query_ref[...] * jnp.bfloat16(HD**-0.5)).T
    value_t = value_ref[...].T
    distance = lax.broadcasted_iota(jnp.int32, (taken, rows), 1) - MIDDLE_DILATION * (
        lax.broadcasted_iota(jnp.int32, (taken, rows), 0)
    )
    near, far = [], []

    def pick(one):
        span = slice(one * HD, (one + 1) * HD)
        for level in range(2):
            select[one, level * taken : (level + 1) * taken] = jnp.where(
                distance == offset_refs[level][one], jnp.float32(1), jnp.float32(0)
            ).astype(jnp.bfloat16)
        chosen = select[one]
        both_t = lax.dot_general(
            jnp.concatenate([value_t[span], query_t[span]], axis=0),
            chosen,
            (((1,), (1,)), ((), ())),
            preferred_element_type=jnp.float32,
        ).astype(jnp.bfloat16)
        picked = dot_f32(chosen, key_ref[:, span]).astype(jnp.bfloat16)
        for level in range(2):
            lanes = slice(level * taken, (level + 1) * taken)
            first = 2 * HD * level
            message[one, first : first + HD] = both_t[:HD, lanes]
            message[one, first + HD : first + 2 * HD] = jnp.concatenate(
                [
                    picked[level * taken : level * taken + taken // 2],
                    picked[level * taken + taken // 2 : (level + 1) * taken],
                ],
                axis=1,
            )
            message[one, (4 + level) * HD : (5 + level) * HD] = both_t[HD:, lanes]

    def send_picked(one):
        slot = lax.rem(one - place + heads, heads)
        far.append(
            pltpu.make_async_remote_copy(
                src_ref=message.at[one, 0 : 4 * HD],
                dst_ref=got.at[heads + slot, 0 : 4 * HD],
                send_sem=send_pick.at[heads + one],
                recv_sem=recv_pick.at[heads + slot],
                device_id=((1 - half) * heads + one, head),
                device_id_type=MESH,
            )
        )
        far[-1].start()
        near.append(
            pltpu.make_async_remote_copy(
                src_ref=message.at[one],
                dst_ref=got.at[slot],
                send_sem=send_pick.at[one],
                recv_sem=recv_pick.at[slot],
                device_id=(half * heads + one, head),
                device_id_type=MESH,
            )
        )
        pl.when(one != place)(near[-1].start)

    for one in range(heads // 2):
        pick(one)
    pl.semaphore_wait(barrier, seq_total + 2)
    for one in range(heads // 2):
        send_picked(one)
    for one in range(heads // 2, heads):
        pick(one)
    for one in range(heads // 2, heads):
        send_picked(one)
    got[0] = message[place]
    loads[5].wait()

    def weight_copy(source, slot, peer):
        return pltpu.make_async_remote_copy(
            src_ref=source,
            dst_ref=weights_got.at[slot],
            send_sem=send_weight.at[slot],
            recv_sem=recv_weight.at[slot],
            device_id=(seq, peers[peer]),
            device_id_type=MESH,
        )

    across = weight_copy(weight_ref, 2, 2)
    across.start()
    beside = weight_copy(weight_ref, 1, 1)
    beside.start()

    cut = rows // 2
    for one in range(heads):
        span = slice(one * HD, (one + 1) * HD)
        for part in range(2):
            lanes = slice(part * cut, (part + 1) * cut)
            scores = dot_f32(key_ref[:, span], query_t[span, lanes])
            row_max = jnp.max(scores, axis=0, keepdims=True)
            mass = jnp.exp(scores - row_max)
            bottom_stats[one, 0:1, lanes] = row_max
            bottom_stats[one, 1:2, lanes] = jnp.sum(mass, axis=0, keepdims=True)
            bottom[one, :, lanes] = dot_f32(value_t[span], mass.astype(jnp.bfloat16))

    for slot in range(1, 2 * heads):
        deep = 6 * HD if slot < heads else 4 * HD
        pltpu.make_async_remote_copy(
            src_ref=message.at[0, 0:deep],
            dst_ref=got.at[slot, 0:deep],
            send_sem=send_pick.at[slot],
            recv_sem=recv_pick.at[slot],
            device_id=(lax.rem(seq + 1, seq_total), head),
            device_id_type=MESH,
        ).wait_recv()

    backs = []
    for slots in ((1, 2), (3, 0)):
        weighted, stats = [], []
        for level in range(2):
            first = 2 * HD * level
            values_t = jnp.concatenate(
                [got[i, first : first + HD] for i in range(seq_total)], axis=1
            )
            keys = jnp.concatenate(
                [got[i, first + HD : first + 2 * HD] for i in range(seq_total)], axis=0
            )
            block = jnp.concatenate(
                [got[i, (4 + level) * HD : (5 + level) * HD] for i in slots], axis=1
            )
            blank = jnp.zeros_like(block)
            left = dot_f32(keys, jnp.concatenate([block, blank], axis=0))
            right = dot_f32(keys, jnp.concatenate([blank, block], axis=0))
            row_max = jnp.maximum(
                jnp.max(left, axis=0, keepdims=True), jnp.max(right, axis=0, keepdims=True)
            )
            left = jnp.exp(left - row_max)
            right = jnp.exp(right - row_max)
            total = jnp.sum(left, axis=0, keepdims=True) + jnp.sum(
                right, axis=0, keepdims=True
            )
            left = left.astype(jnp.bfloat16)
            right = right.astype(jnp.bfloat16)
            pieces = []
            for i in range(seq_total):
                pieces.append(left[i * HD : (i + 1) * HD])
                pieces.append(right[i * HD : (i + 1) * HD])
            weighted.append(dot_f32(values_t, jnp.concatenate(pieces, axis=0)))
            stats += three_parts(row_max) + three_parts(total)
        stats.append(jnp.zeros((STAT_ROWS - len(stats), 2 * taken), jnp.float32))
        packed = jnp.concatenate(weighted + stats, axis=0).astype(jnp.bfloat16)
        for step, begin in zip(slots, (0, taken)):
            if step == 0:
                returned[place] = packed[:, begin : begin + taken]
                continue
            result[step] = packed[:, begin : begin + taken]
            backs.append(
                pltpu.make_async_remote_copy(
                    src_ref=result.at[step],
                    dst_ref=returned.at[place],
                    send_sem=send_back.at[step],
                    recv_sem=recv_back.at[step],
                    device_id=(half * heads + lax.rem(place - step + heads, heads), head),
                    device_id_type=MESH,
                )
            )
            backs[-1].start()

    across.wait_recv()
    onward = weight_copy(weights_got.at[2], 3, 1)
    onward.start()

    for step in range(1, heads):
        source = lax.rem(place + step, heads)
        pltpu.make_async_remote_copy(
            src_ref=result.at[step],
            dst_ref=returned.at[source],
            send_sem=send_back.at[step],
            recv_sem=recv_back.at[step],
            device_id=(half * heads + source, head),
            device_id_type=MESH,
        ).wait_recv()
    residue = lax.rem(lax.broadcasted_iota(jnp.int32, (1, rows), 1), MIDDLE_DILATION)
    for one in range(heads):
        maxima = [bottom_stats[one, 0:1]]
        totals = [bottom_stats[one, 1:2]]
        sums = [bottom[one]]
        for level in range(2):
            lines = slice(level * taken, (level + 1) * taken)
            spread = dot_f32(returned[one, level * HD : (level + 1) * HD], select[one, lines])
            stats = dot_f32(returned[one, 2 * HD :], select[one, lines])[6 * level :]
            row_max = stats[0:1] + stats[1:2] + stats[2:3]
            maxima.append(
                jnp.where(residue == offset_refs[level][one], row_max, -jnp.inf)
            )
            totals.append(stats[3:4] + stats[4:5] + stats[5:6])
            sums.append(spread)
        highest = jnp.maximum(jnp.maximum(maxima[0], maxima[1]), maxima[2])
        factors = [jnp.exp(row_max - highest) for row_max in maxima]
        denominator = sum(f * t for f, t in zip(factors, totals))
        inverse = 1.0 / denominator
        attention = sum((f * inverse) * w for f, w in zip(factors, sums)).astype(
            jnp.bfloat16
        )
        for i in range(4):
            columns[i, one * HD : (one + 1) * HD] = attention[
                :, i * taken : (i + 1) * taken
            ]

    sent = []
    for step in range(1, 4):
        sent.append(
            pltpu.make_async_remote_copy(
                src_ref=columns.at[peers[step]],
                dst_ref=columns_got.at[step],
                send_sem=send_columns.at[step],
                recv_sem=recv_columns.at[step],
                device_id=(seq, peers[step]),
                device_id_type=MESH,
            )
        )
        sent[-1].start()
    projected = dot_f32(columns[head].T, weight_ref[...])
    for step, weight in ((1, beside), (2, None), (3, onward)):
        if weight is not None:
            weight.wait_recv()
        sent[step - 1].wait_recv()
        projected += dot_f32(columns_got[step].T, weights_got[step])
    out_ref[...] = projected.astype(out_ref.dtype)
    for one in range(heads):
        pl.when(one != place)(near[one].wait_send)
    for copy in far + backs + sent + [across, beside, onward]:
        copy.wait_send()


def per_device_fused(query, key, value, middle_offsets, upper_offsets, out_weight):
    rows, width = query.shape
    seq_total = lax.axis_size("seq")
    heads = width // HD
    taken = rows // MIDDLE_DILATION
    whole = pl.BlockSpec(memory_space=pltpu.VMEM)
    anywhere = pl.BlockSpec(memory_space=pl.ANY)
    dma = pltpu.SemaphoreType.DMA
    return pl.pallas_call(
        functools.partial(fused_kernel, seq_total),
        out_shape=jax.ShapeDtypeStruct((rows // 4, out_weight.shape[1]), jnp.bfloat16),
        in_specs=[anywhere] * 6,
        out_specs=whole,
        scratch_shapes=[
            pltpu.VMEM(query.shape, query.dtype),
            pltpu.VMEM(key.shape, key.dtype),
            pltpu.VMEM(value.shape, value.dtype),
            pltpu.SMEM(middle_offsets.shape, jnp.int32),
            pltpu.SMEM(upper_offsets.shape, jnp.int32),
            pltpu.VMEM(out_weight.shape, out_weight.dtype),
            dma((6,)),
            pltpu.VMEM((heads, 2 * taken, rows), jnp.bfloat16),
            pltpu.VMEM((heads, 6 * HD, taken), jnp.bfloat16),
            pltpu.VMEM((seq_total, 6 * HD, taken), jnp.bfloat16),
            pltpu.VMEM((heads, 2 * HD + STAT_ROWS, taken), jnp.bfloat16),
            pltpu.VMEM((heads, 2 * HD + STAT_ROWS, taken), jnp.bfloat16),
            pltpu.VMEM((heads, HD, rows), jnp.float32),
            pltpu.VMEM((heads, 8, rows), jnp.float32),
            pltpu.VMEM((4, width, taken), jnp.bfloat16),
            pltpu.VMEM((4, width, taken), jnp.bfloat16),
            pltpu.VMEM((4,) + out_weight.shape, jnp.bfloat16),
            dma((seq_total,)),
            dma((seq_total,)),
            dma((seq_total,)),
            dma((seq_total,)),
            dma((4,)),
            dma((4,)),
            dma((4,)),
            dma((4,)),
        ],
        compiler_params=pltpu.CompilerParams(
            collective_id=0, has_side_effects=True, vmem_limit_bytes=60 * 2**20
        ),
    )(query, key, value, middle_offsets, upper_offsets, out_weight)


def solution(mesh):
    in_specs = (
        P("seq", "head"),
        P("seq", "head"),
        P("seq", "head"),
        P("head"),
        P("head"),
        P("head", None),
    )
    out_specs = P(("seq", "head"), None)
    seq_total, head_shards = mesh.shape["seq"], mesh.shape["head"]
    one_segment = seq_total == SPAN and seq_total // 2 == MIDDLE_DILATION and head_shards == 4
    return jax.shard_map(
        per_device_fused if one_segment else per_device, mesh=mesh, in_specs=in_specs, out_specs=out_specs, check_vma=False
    )
```

```python
import functools

import jax
import jax.numpy as jnp
from jax import lax
from jax.experimental import pallas as pl
from jax.experimental.pallas import tpu as pltpu
from jax.sharding import PartitionSpec as P

HD = 64
SPAN = 8
MIDDLE_DILATION = 4


def partner_2(value, axis, stride):
    mask = 2**stride
    pairs = [(source, source ^ mask) for source in range(lax.axis_size(axis))]
    return lax.ppermute(value, axis, pairs)


def attend_segment(query_matrix_rows, key_matrix_rows, value_matrix_rows):
    scores = jnp.einsum(
        "qhd,khd->hqk", query_matrix_rows, key_matrix_rows, preferred_element_type=jnp.float32
    ) * HD ** (-0.5)
    row_max = jnp.max(scores, axis=2)
    mass = jnp.exp(scores - row_max[:, :, None])
    total = jnp.sum(mass, axis=2)
    soft_weights = mass.astype(jnp.bfloat16)
    weighted = jnp.einsum(
        "hqk,khd->qhd", soft_weights, value_matrix_rows, preferred_element_type=jnp.float32
    )
    return (weighted, total.T, row_max.T)


def attend_blocks(query_matrix_rows, key_matrix_rows, value_matrix_rows):
    block_size = min(512, query_matrix_rows.shape[0])
    pieces = query_matrix_rows.reshape(
        query_matrix_rows.shape[0] // block_size,
        block_size,
        query_matrix_rows.shape[1],
        query_matrix_rows.shape[2],
    )

    def one_block(one_piece):
        return attend_segment(one_piece, key_matrix_rows, value_matrix_rows)

    weighted, total, row_max = lax.map(one_block, pieces)
    return (
        weighted.reshape(query_matrix_rows.shape),
        total.reshape(query_matrix_rows.shape[:2]),
        row_max.reshape(query_matrix_rows.shape[:2]),
    )


def picked_rows(block_rows, offsets, stride):
    group_count = block_rows.shape[0] // stride
    grouped = block_rows.reshape(group_count, stride, block_rows.shape[1], block_rows.shape[2])
    chosen = (
        jnp.arange(stride, dtype=jnp.int32)[None, :, None, None] == offsets[None, None, :, None]
    )
    return jnp.sum(jnp.where(chosen, grouped, jnp.zeros((), grouped.dtype)), axis=1)


def scatter_rows(values, offsets, stride, filler):
    chosen = jnp.arange(stride, dtype=jnp.int32)[:, None] == offsets[None, :]
    spread_out = jnp.where(chosen[None], values[:, None], filler)
    return spread_out.reshape((values.shape[0] * stride,) + values.shape[1:])


def flatten_level(result):
    row_total = result[0].shape[0]
    weighted = result[0].reshape(row_total, -1)
    total = jnp.repeat(result[1], HD, axis=1)
    row_max = jnp.repeat(result[2], HD, axis=1)
    return (weighted, total, row_max)


def scatter_level(result, offsets, stride):
    weighted, total, row_max = flatten_level(result)
    column_offsets = jnp.repeat(offsets, HD)
    return (
        scatter_rows(weighted, column_offsets, stride, 0.0),
        scatter_rows(total, column_offsets, stride, 0.0),
        scatter_rows(row_max, column_offsets, stride, -jnp.inf),
    )


def combine(levels):
    highest = levels[0][2]
    for one_level in levels[1:]:
        highest = jnp.maximum(highest, one_level[2])
    numerator = jnp.zeros(levels[0][0].shape, jnp.float32)
    denominator = jnp.zeros(levels[0][1].shape, jnp.float32)
    for one_level in levels:
        factor = jnp.exp(one_level[2] - highest)
        numerator = numerator + factor * one_level[0]
        denominator = denominator + factor * one_level[1]
    return (numerator / denominator).astype(jnp.bfloat16)


def per_device(query, key, value, middle_offsets, upper_offsets, out_weight):
    row_count = query.shape[0]
    head_count = query.shape[1] // HD
    top_stride = lax.axis_size("seq") // 2
    query_matrix_rows = query.reshape(row_count, head_count, HD)
    key_matrix_rows = key.reshape(row_count, head_count, HD)
    value_matrix_rows = value.reshape(row_count, head_count, HD)
    top_key_local = picked_rows(key_matrix_rows, upper_offsets, top_stride).reshape(
        -1, head_count * HD
    )
    top_value_local = picked_rows(value_matrix_rows, upper_offsets, top_stride).reshape(
        -1, head_count * HD
    )
    top_key_all, top_value_all = (
        lax.all_gather(top_key_local, "seq", axis=0, tiled=True),
        lax.all_gather(top_value_local, "seq", axis=0, tiled=True),
    )
    upper_level = attend_segment(
        picked_rows(query_matrix_rows, upper_offsets, top_stride),
        top_key_all.reshape(-1, head_count, HD),
        top_value_all.reshape(-1, head_count, HD),
    )
    middle_pair = jnp.stack(
        [
            picked_rows(key_matrix_rows, middle_offsets, MIDDLE_DILATION),
            picked_rows(value_matrix_rows, middle_offsets, MIDDLE_DILATION),
        ]
    ).reshape(2, -1, head_count * HD)
    for bit_number in range(SPAN.bit_length() - 1):
        partner = partner_2(middle_pair, "seq", bit_number)
        middle_pair = jnp.concatenate([middle_pair, partner], axis=1)
    middle_level = attend_segment(
        picked_rows(query_matrix_rows, middle_offsets, MIDDLE_DILATION),
        middle_pair[0].reshape(-1, head_count, HD),
        middle_pair[1].reshape(-1, head_count, HD),
    )
    bottom = flatten_level(attend_blocks(query_matrix_rows, key_matrix_rows, value_matrix_rows))
    attention = combine(
        (
            bottom,
            scatter_level(middle_level, middle_offsets, MIDDLE_DILATION),
            scatter_level(upper_level, upper_offsets, top_stride),
        )
    )
    summed = lax.psum_scatter(
        jnp.dot(attention, out_weight, preferred_element_type=jnp.float32),
        "head",
        scatter_dimension=0,
        tiled=True,
    )
    return summed.astype(jnp.bfloat16)


MESH = pl.DeviceIdType.MESH
STAT_ROWS = 16


def dot_f32(left, right):
    return jnp.dot(left, right, preferred_element_type=jnp.float32)


def three_parts(value):
    high = value.astype(jnp.bfloat16).astype(jnp.float32)
    rest = value - high
    middle = rest.astype(jnp.bfloat16).astype(jnp.float32)
    return [high, middle, rest - middle]


def fused_kernel(
    seq_total,
    query_hbm,
    key_hbm,
    value_hbm,
    middle_hbm,
    upper_hbm,
    weight_hbm,
    out_ref,
    query_ref,
    key_ref,
    value_ref,
    middle_ref,
    upper_ref,
    weight_ref,
    load,
    select,
    message,
    got,
    result,
    returned,
    bottom,
    bottom_stats,
    columns,
    columns_got,
    weights_got,
    send_pick,
    recv_pick,
    send_back,
    recv_back,
    send_columns,
    recv_columns,
    send_weight,
    recv_weight,
):
    seq, head = lax.axis_index("seq"), lax.axis_index("head")
    chip, core = lax.div(head, 2), lax.rem(head, 2)
    peers = [
        head,
        2 * chip + (1 - core),
        2 * (1 - chip) + core,
        2 * (1 - chip) + (1 - core),
    ]
    rows = query_ref.shape[0]
    heads = query_ref.shape[1] // HD
    taken = rows // MIDDLE_DILATION
    offset_refs = (middle_ref, upper_ref)

    loads = []
    for i, (source, target) in enumerate(
        (
            (middle_hbm, middle_ref),
            (upper_hbm, upper_ref),
            (query_hbm, query_ref),
            (value_hbm, value_ref),
            (key_hbm, key_ref),
            (weight_hbm, weight_ref),
        )
    ):
        loads.append(pltpu.make_async_copy(source, target, load.at[i]))
        loads[-1].start()

    barrier = pltpu.get_barrier_semaphore()
    for step in range(1, seq_total):
        pl.semaphore_signal(
            barrier,
            inc=1,
            device_id=(lax.rem(seq + step, seq_total), head),
            device_id_type=MESH,
        )
    for step in range(1, 4):
        pl.semaphore_signal(
            barrier, inc=1, device_id=(seq, peers[step]), device_id_type=MESH
        )

    for copy in loads[:5]:
        copy.wait()
    query_t = (query_ref[...] * jnp.bfloat16(HD**-0.5)).T
    value_t = value_ref[...].T
    distance = lax.broadcasted_iota(jnp.int32, (taken, rows), 1) - MIDDLE_DILATION * (
        lax.broadcasted_iota(jnp.int32, (taken, rows), 0)
    )
    picks = {}

    def pick(one):
        span = slice(one * HD, (one + 1) * HD)
        both_t = jnp.concatenate([query_t[span], value_t[span]], axis=0)
        for level in range(2):
            pair = level * heads + one
            chosen = jnp.where(
                distance == offset_refs[level][one], jnp.float32(1), jnp.float32(0)
            ).astype(jnp.bfloat16)
            select[pair] = chosen
            message[pair, 0 : 2 * HD] = lax.dot_general(
                both_t,
                chosen,
                (((1,), (1,)), ((), ())),
                preferred_element_type=jnp.float32,
            ).astype(jnp.bfloat16)
            picked = dot_f32(chosen, key_ref[:, span])
            message[pair, 2 * HD : 3 * HD] = jnp.concatenate(
                [picked[: taken // 2], picked[taken // 2 :]], axis=1
            ).astype(jnp.bfloat16)

    def send_picked(pair):
        slot = lax.rem(pair - seq + seq_total, seq_total)
        picks[pair] = pltpu.make_async_remote_copy(
            src_ref=message.at[pair],
            dst_ref=got.at[slot],
            send_sem=send_pick.at[pair],
            recv_sem=recv_pick.at[slot],
            device_id=(pair, head),
            device_id_type=MESH,
        )
        pl.when(pair != seq)(picks[pair].start)

    for begin in range(0, heads, 2):
        for one in (begin, begin + 1):
            pick(one)
        if begin == 0:
            pl.semaphore_wait(barrier, seq_total + 2)
        for one in (begin, begin + 1):
            for level in range(2):
                send_picked(level * heads + one)
    got[0] = message[seq]

    loads[5].wait()

    def weight_copy(source, slot, peer):
        return pltpu.make_async_remote_copy(
            src_ref=source,
            dst_ref=weights_got.at[slot],
            send_sem=send_weight.at[slot],
            recv_sem=recv_weight.at[slot],
            device_id=(seq, peers[peer]),
            device_id_type=MESH,
        )

    across = weight_copy(weight_ref, 2, 2)
    across.start()
    beside = weight_copy(weight_ref, 1, 1)
    beside.start()

    half = rows // 2
    for one in range(heads):
        span = slice(one * HD, (one + 1) * HD)
        for part in range(2):
            lanes = slice(part * half, (part + 1) * half)
            scores = dot_f32(key_ref[:, span], query_t[span, lanes])
            row_max = jnp.max(scores, axis=0, keepdims=True)
            mass = jnp.exp(scores - row_max)
            bottom_stats[one, 0:1, lanes] = row_max
            bottom_stats[one, 1:2, lanes] = jnp.sum(mass, axis=0, keepdims=True)
            bottom[one, :, lanes] = dot_f32(value_t[span], mass.astype(jnp.bfloat16))

    for slot in range(1, seq_total):
        pltpu.make_async_remote_copy(
            src_ref=message.at[0],
            dst_ref=got.at[slot],
            send_sem=send_pick.at[0],
            recv_sem=recv_pick.at[slot],
            device_id=(lax.rem(seq + 1, seq_total), head),
            device_id_type=MESH,
        ).wait_recv()
    keys = jnp.concatenate([got[i, 2 * HD : 3 * HD] for i in range(seq_total)], axis=0)
    values_t = jnp.concatenate([got[i, HD : 2 * HD] for i in range(seq_total)], axis=1)
    backs = []
    middle = seq_total // 2
    for i in range(middle):
        slots = (middle - i, (middle + 1 + i) % seq_total)
        block = jnp.concatenate([got[slot, 0:HD] for slot in slots], axis=1)
        blank = jnp.zeros_like(block)
        first = dot_f32(keys, jnp.concatenate([block, blank], axis=0))
        second = dot_f32(keys, jnp.concatenate([blank, block], axis=0))
        row_max = jnp.maximum(
            jnp.max(first, axis=0, keepdims=True), jnp.max(second, axis=0, keepdims=True)
        )
        first = jnp.exp(first - row_max)
        second = jnp.exp(second - row_max)
        total = jnp.sum(first, axis=0, keepdims=True) + jnp.sum(
            second, axis=0, keepdims=True
        )
        first = first.astype(jnp.bfloat16)
        second = second.astype(jnp.bfloat16)
        pieces = []
        for i in range(seq_total):
            pieces.append(first[i * HD : (i + 1) * HD])
            pieces.append(second[i * HD : (i + 1) * HD])
        weighted = dot_f32(values_t, jnp.concatenate(pieces, axis=0))
        stats = three_parts(row_max) + three_parts(total)
        stats.append(jnp.zeros((STAT_ROWS - len(stats), 2 * taken), jnp.float32))
        packed = jnp.concatenate([weighted] + stats, axis=0).astype(jnp.bfloat16)
        for step, begin in zip(slots, (0, taken)):
            result[step] = packed[:, begin : begin + taken]
            if step == 0:
                returned[seq] = packed[:, begin : begin + taken]
                continue
            backs.append(
                pltpu.make_async_remote_copy(
                    src_ref=result.at[step],
                    dst_ref=returned.at[seq],
                    send_sem=send_back.at[step],
                    recv_sem=recv_back.at[step],
                    device_id=(lax.rem(seq - step + seq_total, seq_total), head),
                    device_id_type=MESH,
                )
            )
            backs[-1].start()

    across.wait_recv()
    onward = weight_copy(weights_got.at[2], 3, 1)
    onward.start()

    for step in range(1, seq_total):
        pltpu.make_async_remote_copy(
            src_ref=result.at[step],
            dst_ref=returned.at[lax.rem(seq + step, seq_total)],
            send_sem=send_back.at[step],
            recv_sem=recv_back.at[step],
            device_id=(lax.rem(seq + step, seq_total), head),
            device_id_type=MESH,
        ).wait_recv()
    residue = lax.rem(lax.broadcasted_iota(jnp.int32, (1, rows), 1), MIDDLE_DILATION)
    for one in range(heads):
        maxima = [bottom_stats[one, 0:1]]
        totals = [bottom_stats[one, 1:2]]
        sums = [bottom[one]]
        for level in range(2):
            pair = level * heads + one
            spread = dot_f32(returned[pair], select[pair])
            row_max = spread[HD : HD + 1] + spread[HD + 1 : HD + 2] + spread[HD + 2 : HD + 3]
            maxima.append(
                jnp.where(residue == offset_refs[level][one], row_max, -jnp.inf)
            )
            totals.append(
                spread[HD + 3 : HD + 4] + spread[HD + 4 : HD + 5] + spread[HD + 5 : HD + 6]
            )
            sums.append(spread[0:HD])
        highest = jnp.maximum(jnp.maximum(maxima[0], maxima[1]), maxima[2])
        factors = [jnp.exp(row_max - highest) for row_max in maxima]
        denominator = sum(f * t for f, t in zip(factors, totals))
        inverse = 1.0 / denominator
        attention = sum((f * inverse) * w for f, w in zip(factors, sums)).astype(
            jnp.bfloat16
        )
        for i in range(4):
            columns[i, one * HD : (one + 1) * HD] = attention[
                :, i * taken : (i + 1) * taken
            ]

    sent = []
    for step in range(1, 4):
        sent.append(
            pltpu.make_async_remote_copy(
                src_ref=columns.at[peers[step]],
                dst_ref=columns_got.at[step],
                send_sem=send_columns.at[step],
                recv_sem=recv_columns.at[step],
                device_id=(seq, peers[step]),
                device_id_type=MESH,
            )
        )
        sent[-1].start()
    projected = dot_f32(columns[head].T, weight_ref[...])
    for step, weight in ((1, beside), (2, None), (3, onward)):
        if weight is not None:
            weight.wait_recv()
        sent[step - 1].wait_recv()
        projected += dot_f32(columns_got[step].T, weights_got[step])
    out_ref[...] = projected.astype(out_ref.dtype)
    for pair in range(seq_total):
        pl.when(pair != seq)(picks[pair].wait_send)
    for copy in backs + sent + [across, beside, onward]:
        copy.wait_send()


def per_device_fused(query, key, value, middle_offsets, upper_offsets, out_weight):
    rows, width = query.shape
    seq_total = lax.axis_size("seq")
    heads = width // HD
    pairs = 2 * heads
    taken = rows // MIDDLE_DILATION
    whole = pl.BlockSpec(memory_space=pltpu.VMEM)
    anywhere = pl.BlockSpec(memory_space=pl.ANY)
    dma = pltpu.SemaphoreType.DMA
    return pl.pallas_call(
        functools.partial(fused_kernel, seq_total),
        out_shape=jax.ShapeDtypeStruct((rows // 4, out_weight.shape[1]), jnp.bfloat16),
        in_specs=[anywhere] * 6,
        out_specs=whole,
        scratch_shapes=[
            pltpu.VMEM(query.shape, query.dtype),
            pltpu.VMEM(key.shape, key.dtype),
            pltpu.VMEM(value.shape, value.dtype),
            pltpu.SMEM(middle_offsets.shape, jnp.int32),
            pltpu.SMEM(upper_offsets.shape, jnp.int32),
            pltpu.VMEM(out_weight.shape, out_weight.dtype),
            dma((6,)),
            pltpu.VMEM((pairs, taken, rows), jnp.bfloat16),
            pltpu.VMEM((pairs, 3 * HD, taken), jnp.bfloat16),
            pltpu.VMEM((seq_total, 3 * HD, taken), jnp.bfloat16),
            pltpu.VMEM((seq_total, HD + STAT_ROWS, taken), jnp.bfloat16),
            pltpu.VMEM((pairs, HD + STAT_ROWS, taken), jnp.bfloat16),
            pltpu.VMEM((heads, HD, rows), jnp.float32),
            pltpu.VMEM((heads, 8, rows), jnp.float32),
            pltpu.VMEM((4, width, taken), jnp.bfloat16),
            pltpu.VMEM((4, width, taken), jnp.bfloat16),
            pltpu.VMEM((4,) + out_weight.shape, jnp.bfloat16),
            dma((seq_total,)),
            dma((seq_total,)),
            dma((seq_total,)),
            dma((seq_total,)),
            dma((4,)),
            dma((4,)),
            dma((4,)),
            dma((4,)),
        ],
        compiler_params=pltpu.CompilerParams(
            collective_id=0, has_side_effects=True, vmem_limit_bytes=60 * 2**20
        ),
    )(query, key, value, middle_offsets, upper_offsets, out_weight)


def solution(mesh):
    in_specs = (
        P("seq", "head"),
        P("seq", "head"),
        P("seq", "head"),
        P("head"),
        P("head"),
        P("head", None),
    )
    out_specs = P(("seq", "head"), None)
    seq_total, head_shards = mesh.shape["seq"], mesh.shape["head"]
    one_segment = seq_total == SPAN and seq_total // 2 == MIDDLE_DILATION and head_shards == 4
    return jax.shard_map(
        per_device_fused if one_segment else per_device, mesh=mesh, in_specs=in_specs, out_specs=out_specs, check_vma=False
    )
```

```python
import functools

import jax
import jax.numpy as jnp
from jax import lax
from jax.experimental import pallas as pl
from jax.experimental.pallas import tpu as pltpu
from jax.sharding import PartitionSpec as P

HD = 64
SPAN = 8
MIDDLE_DILATION = 4


def partner_2(value, axis, stride):
    mask = 2**stride
    pairs = [(source, source ^ mask) for source in range(lax.axis_size(axis))]
    return lax.ppermute(value, axis, pairs)


def attend_segment(query_matrix_rows, key_matrix_rows, value_matrix_rows):
    scores = jnp.einsum(
        "qhd,khd->hqk", query_matrix_rows, key_matrix_rows, preferred_element_type=jnp.float32
    ) * HD ** (-0.5)
    row_max = jnp.max(scores, axis=2)
    mass = jnp.exp(scores - row_max[:, :, None])
    total = jnp.sum(mass, axis=2)
    soft_weights = mass.astype(jnp.bfloat16)
    weighted = jnp.einsum(
        "hqk,khd->qhd", soft_weights, value_matrix_rows, preferred_element_type=jnp.float32
    )
    return (weighted, total.T, row_max.T)


def attend_blocks(query_matrix_rows, key_matrix_rows, value_matrix_rows):
    block_size = min(512, query_matrix_rows.shape[0])
    pieces = query_matrix_rows.reshape(
        query_matrix_rows.shape[0] // block_size,
        block_size,
        query_matrix_rows.shape[1],
        query_matrix_rows.shape[2],
    )

    def one_block(one_piece):
        return attend_segment(one_piece, key_matrix_rows, value_matrix_rows)

    weighted, total, row_max = lax.map(one_block, pieces)
    return (
        weighted.reshape(query_matrix_rows.shape),
        total.reshape(query_matrix_rows.shape[:2]),
        row_max.reshape(query_matrix_rows.shape[:2]),
    )


def picked_rows(block_rows, offsets, stride):
    group_count = block_rows.shape[0] // stride
    grouped = block_rows.reshape(group_count, stride, block_rows.shape[1], block_rows.shape[2])
    chosen = (
        jnp.arange(stride, dtype=jnp.int32)[None, :, None, None] == offsets[None, None, :, None]
    )
    return jnp.sum(jnp.where(chosen, grouped, jnp.zeros((), grouped.dtype)), axis=1)


def scatter_rows(values, offsets, stride, filler):
    chosen = jnp.arange(stride, dtype=jnp.int32)[:, None] == offsets[None, :]
    spread_out = jnp.where(chosen[None], values[:, None], filler)
    return spread_out.reshape((values.shape[0] * stride,) + values.shape[1:])


def flatten_level(result):
    row_total = result[0].shape[0]
    weighted = result[0].reshape(row_total, -1)
    total = jnp.repeat(result[1], HD, axis=1)
    row_max = jnp.repeat(result[2], HD, axis=1)
    return (weighted, total, row_max)


def scatter_level(result, offsets, stride):
    weighted, total, row_max = flatten_level(result)
    column_offsets = jnp.repeat(offsets, HD)
    return (
        scatter_rows(weighted, column_offsets, stride, 0.0),
        scatter_rows(total, column_offsets, stride, 0.0),
        scatter_rows(row_max, column_offsets, stride, -jnp.inf),
    )


def combine(levels):
    highest = levels[0][2]
    for one_level in levels[1:]:
        highest = jnp.maximum(highest, one_level[2])
    numerator = jnp.zeros(levels[0][0].shape, jnp.float32)
    denominator = jnp.zeros(levels[0][1].shape, jnp.float32)
    for one_level in levels:
        factor = jnp.exp(one_level[2] - highest)
        numerator = numerator + factor * one_level[0]
        denominator = denominator + factor * one_level[1]
    return (numerator / denominator).astype(jnp.bfloat16)


def per_device(query, key, value, middle_offsets, upper_offsets, out_weight):
    row_count = query.shape[0]
    head_count = query.shape[1] // HD
    top_stride = lax.axis_size("seq") // 2
    query_matrix_rows = query.reshape(row_count, head_count, HD)
    key_matrix_rows = key.reshape(row_count, head_count, HD)
    value_matrix_rows = value.reshape(row_count, head_count, HD)
    top_key_local = picked_rows(key_matrix_rows, upper_offsets, top_stride).reshape(
        -1, head_count * HD
    )
    top_value_local = picked_rows(value_matrix_rows, upper_offsets, top_stride).reshape(
        -1, head_count * HD
    )
    top_key_all, top_value_all = (
        lax.all_gather(top_key_local, "seq", axis=0, tiled=True),
        lax.all_gather(top_value_local, "seq", axis=0, tiled=True),
    )
    upper_level = attend_segment(
        picked_rows(query_matrix_rows, upper_offsets, top_stride),
        top_key_all.reshape(-1, head_count, HD),
        top_value_all.reshape(-1, head_count, HD),
    )
    middle_pair = jnp.stack(
        [
            picked_rows(key_matrix_rows, middle_offsets, MIDDLE_DILATION),
            picked_rows(value_matrix_rows, middle_offsets, MIDDLE_DILATION),
        ]
    ).reshape(2, -1, head_count * HD)
    for bit_number in range(SPAN.bit_length() - 1):
        partner = partner_2(middle_pair, "seq", bit_number)
        middle_pair = jnp.concatenate([middle_pair, partner], axis=1)
    middle_level = attend_segment(
        picked_rows(query_matrix_rows, middle_offsets, MIDDLE_DILATION),
        middle_pair[0].reshape(-1, head_count, HD),
        middle_pair[1].reshape(-1, head_count, HD),
    )
    bottom = flatten_level(attend_blocks(query_matrix_rows, key_matrix_rows, value_matrix_rows))
    attention = combine(
        (
            bottom,
            scatter_level(middle_level, middle_offsets, MIDDLE_DILATION),
            scatter_level(upper_level, upper_offsets, top_stride),
        )
    )
    summed = lax.psum_scatter(
        jnp.dot(attention, out_weight, preferred_element_type=jnp.float32),
        "head",
        scatter_dimension=0,
        tiled=True,
    )
    return summed.astype(jnp.bfloat16)


MESH = pl.DeviceIdType.MESH
STAT_ROWS = 16


def dot_f32(left, right):
    return jnp.dot(left, right, preferred_element_type=jnp.float32)


def three_parts(value):
    high = value.astype(jnp.bfloat16).astype(jnp.float32)
    rest = value - high
    middle = rest.astype(jnp.bfloat16).astype(jnp.float32)
    return [high, middle, rest - middle]


def fused_kernel(
    seq_total,
    query_hbm,
    key_hbm,
    value_hbm,
    middle_hbm,
    upper_hbm,
    weight_hbm,
    out_ref,
    query_ref,
    key_ref,
    value_ref,
    middle_ref,
    upper_ref,
    weight_ref,
    load,
    select,
    message,
    got,
    result,
    returned,
    bottom,
    bottom_stats,
    columns,
    columns_got,
    weights_got,
    send_pick,
    recv_pick,
    send_back,
    recv_back,
    send_columns,
    recv_columns,
    send_weight,
    recv_weight,
):
    seq, head = lax.axis_index("seq"), lax.axis_index("head")
    chip, core = lax.div(head, 2), lax.rem(head, 2)
    peers = [
        head,
        2 * chip + (1 - core),
        2 * (1 - chip) + core,
        2 * (1 - chip) + (1 - core),
    ]
    rows = query_ref.shape[0]
    heads = query_ref.shape[1] // HD
    taken = rows // MIDDLE_DILATION
    offset_refs = (middle_ref, upper_ref)

    barrier = pltpu.get_barrier_semaphore()
    for step in range(1, seq_total):
        pl.semaphore_signal(
            barrier,
            inc=1,
            device_id=(lax.rem(seq + step, seq_total), head),
            device_id_type=MESH,
        )
    for step in range(1, 4):
        pl.semaphore_signal(
            barrier, inc=1, device_id=(seq, peers[step]), device_id_type=MESH
        )

    loads = []
    for i, (source, target) in enumerate(
        (
            (middle_hbm, middle_ref),
            (upper_hbm, upper_ref),
            (query_hbm, query_ref),
            (value_hbm, value_ref),
            (key_hbm, key_ref),
            (weight_hbm, weight_ref),
        )
    ):
        loads.append(pltpu.make_async_copy(source, target, load.at[i]))
        loads[-1].start()

    for copy in loads[:5]:
        copy.wait()
    scale = jnp.bfloat16(HD**-0.5)
    query_t, value_t = {}, {}
    distance = lax.broadcasted_iota(jnp.int32, (taken, rows), 1) - MIDDLE_DILATION * (
        lax.broadcasted_iota(jnp.int32, (taken, rows), 0)
    )
    picks = {}

    def pick(one):
        span = slice(one * HD, (one + 1) * HD)
        both_t = jnp.concatenate([query_t[one], value_t[one]], axis=0)
        for level in range(2):
            pair = level * heads + one
            chosen = jnp.where(
                distance == offset_refs[level][one], jnp.float32(1), jnp.float32(0)
            ).astype(jnp.bfloat16)
            select[pair] = chosen
            message[pair, 0 : 2 * HD] = lax.dot_general(
                both_t,
                chosen,
                (((1,), (1,)), ((), ())),
                preferred_element_type=jnp.float32,
            ).astype(jnp.bfloat16)
            picked = dot_f32(chosen, key_ref[:, span])
            message[pair, 2 * HD : 3 * HD] = jnp.concatenate(
                [picked[: taken // 2], picked[taken // 2 :]], axis=1
            ).astype(jnp.bfloat16)

    def send_picked(pair):
        slot = lax.rem(pair - seq + seq_total, seq_total)
        picks[pair] = pltpu.make_async_remote_copy(
            src_ref=message.at[pair],
            dst_ref=got.at[slot],
            send_sem=send_pick.at[pair],
            recv_sem=recv_pick.at[slot],
            device_id=(pair, head),
            device_id_type=MESH,
        )
        pl.when(pair != seq)(picks[pair].start)

    for begin in range(0, heads, 2):
        span = slice(begin * HD, (begin + 2) * HD)
        query_both = (query_ref[:, span] * scale).T
        value_both = value_ref[:, span].T
        for i in range(2):
            query_t[begin + i] = query_both[i * HD : (i + 1) * HD]
            value_t[begin + i] = value_both[i * HD : (i + 1) * HD]
        for one in (begin, begin + 1):
            pick(one)
            if one == 0:
                pl.semaphore_wait(barrier, seq_total + 2)
            for level in range(2):
                send_picked(level * heads + one)
    got[0] = message[seq]

    loads[5].wait()

    def weight_copy(source, slot, peer):
        return pltpu.make_async_remote_copy(
            src_ref=source,
            dst_ref=weights_got.at[slot],
            send_sem=send_weight.at[slot],
            recv_sem=recv_weight.at[slot],
            device_id=(seq, peers[peer]),
            device_id_type=MESH,
        )

    half = rows // 2
    for one in range(heads):
        span = slice(one * HD, (one + 1) * HD)
        for part in range(2):
            lanes = slice(part * half, (part + 1) * half)
            scores = dot_f32(key_ref[:, span], query_t[one][:, lanes])
            row_max = jnp.max(scores, axis=0, keepdims=True)
            mass = jnp.exp(scores - row_max)
            bottom_stats[one, 0:1, lanes] = row_max
            bottom_stats[one, 1:2, lanes] = jnp.sum(mass, axis=0, keepdims=True)
            bottom[one, :, lanes] = dot_f32(value_t[one], mass.astype(jnp.bfloat16))

    across = weight_copy(weight_ref, 2, 2)
    across.start()
    beside = weight_copy(weight_ref, 1, 1)
    beside.start()

    for slot in range(1, seq_total):
        pltpu.make_async_remote_copy(
            src_ref=message.at[0],
            dst_ref=got.at[slot],
            send_sem=send_pick.at[0],
            recv_sem=recv_pick.at[slot],
            device_id=(lax.rem(seq + 1, seq_total), head),
            device_id_type=MESH,
        ).wait_recv()
    keys = jnp.concatenate([got[i, 2 * HD : 3 * HD] for i in range(seq_total)], axis=0)
    values_t = jnp.concatenate([got[i, HD : 2 * HD] for i in range(seq_total)], axis=1)
    backs = []
    middle = seq_total // 2
    for i in range(middle):
        slots = (middle - i, (middle + 1 + i) % seq_total)
        block = jnp.concatenate([got[slot, 0:HD] for slot in slots], axis=1)
        blank = jnp.zeros_like(block)
        first = dot_f32(keys, jnp.concatenate([block, blank], axis=0))
        second = dot_f32(keys, jnp.concatenate([blank, block], axis=0))
        row_max = jnp.maximum(
            jnp.max(first, axis=0, keepdims=True), jnp.max(second, axis=0, keepdims=True)
        )
        first = jnp.exp(first - row_max)
        second = jnp.exp(second - row_max)
        total = jnp.sum(first, axis=0, keepdims=True) + jnp.sum(
            second, axis=0, keepdims=True
        )
        first = first.astype(jnp.bfloat16)
        second = second.astype(jnp.bfloat16)
        pieces = []
        for i in range(seq_total):
            pieces.append(first[i * HD : (i + 1) * HD])
            pieces.append(second[i * HD : (i + 1) * HD])
        weighted = dot_f32(values_t, jnp.concatenate(pieces, axis=0))
        stats = three_parts(row_max) + three_parts(total)
        stats.append(jnp.zeros((STAT_ROWS - len(stats), 2 * taken), jnp.float32))
        packed = jnp.concatenate([weighted] + stats, axis=0).astype(jnp.bfloat16)
        for step, begin in zip(slots, (0, taken)):
            result[step] = packed[:, begin : begin + taken]
            if step == 0:
                returned[seq] = packed[:, begin : begin + taken]
                continue
            backs.append(
                pltpu.make_async_remote_copy(
                    src_ref=result.at[step],
                    dst_ref=returned.at[seq],
                    send_sem=send_back.at[step],
                    recv_sem=recv_back.at[step],
                    device_id=(lax.rem(seq - step + seq_total, seq_total), head),
                    device_id_type=MESH,
                )
            )
            backs[-1].start()

    across.wait_recv()
    onward = weight_copy(weights_got.at[2], 3, 1)
    onward.start()

    for step in range(1, seq_total):
        pltpu.make_async_remote_copy(
            src_ref=result.at[step],
            dst_ref=returned.at[lax.rem(seq + step, seq_total)],
            send_sem=send_back.at[step],
            recv_sem=recv_back.at[step],
            device_id=(lax.rem(seq + step, seq_total), head),
            device_id_type=MESH,
        ).wait_recv()
    residue = lax.rem(lax.broadcasted_iota(jnp.int32, (1, rows), 1), MIDDLE_DILATION)
    for one in range(heads):
        maxima = [bottom_stats[one, 0:1]]
        totals = [bottom_stats[one, 1:2]]
        sums = [bottom[one]]
        for level in range(2):
            pair = level * heads + one
            spread = dot_f32(returned[pair], select[pair])
            row_max = spread[HD : HD + 1] + spread[HD + 1 : HD + 2] + spread[HD + 2 : HD + 3]
            maxima.append(
                jnp.where(residue == offset_refs[level][one], row_max, -jnp.inf)
            )
            totals.append(
                spread[HD + 3 : HD + 4] + spread[HD + 4 : HD + 5] + spread[HD + 5 : HD + 6]
            )
            sums.append(spread[0:HD])
        highest = jnp.maximum(jnp.maximum(maxima[0], maxima[1]), maxima[2])
        factors = [jnp.exp(row_max - highest) for row_max in maxima]
        denominator = sum(f * t for f, t in zip(factors, totals))
        inverse = 1.0 / denominator
        attention = sum((f * inverse) * w for f, w in zip(factors, sums)).astype(
            jnp.bfloat16
        )
        for i in range(4):
            columns[i, one * HD : (one + 1) * HD] = attention[
                :, i * taken : (i + 1) * taken
            ]

    sent = []
    for step in (2, 3, 1):
        sent.append(
            pltpu.make_async_remote_copy(
                src_ref=columns.at[peers[step]],
                dst_ref=columns_got.at[step],
                send_sem=send_columns.at[step],
                recv_sem=recv_columns.at[step],
                device_id=(seq, peers[step]),
                device_id_type=MESH,
            )
        )
        sent[-1].start()
    projected = dot_f32(columns[head].T, weight_ref[...])
    for step, weight, arriving in (
        (1, beside, sent[2]),
        (2, None, sent[0]),
        (3, onward, sent[1]),
    ):
        if weight is not None:
            weight.wait_recv()
        arriving.wait_recv()
        projected += dot_f32(columns_got[step].T, weights_got[step])
    out_ref[...] = projected.astype(out_ref.dtype)
    for pair in range(seq_total):
        pl.when(pair != seq)(picks[pair].wait_send)
    for copy in backs + sent + [across, beside, onward]:
        copy.wait_send()


def per_device_fused(query, key, value, middle_offsets, upper_offsets, out_weight):
    rows, width = query.shape
    seq_total = lax.axis_size("seq")
    heads = width // HD
    pairs = 2 * heads
    taken = rows // MIDDLE_DILATION
    whole = pl.BlockSpec(memory_space=pltpu.VMEM)
    anywhere = pl.BlockSpec(memory_space=pl.ANY)
    dma = pltpu.SemaphoreType.DMA
    return pl.pallas_call(
        functools.partial(fused_kernel, seq_total),
        out_shape=jax.ShapeDtypeStruct((rows // 4, out_weight.shape[1]), jnp.bfloat16),
        in_specs=[anywhere] * 6,
        out_specs=whole,
        scratch_shapes=[
            pltpu.VMEM(query.shape, query.dtype),
            pltpu.VMEM(key.shape, key.dtype),
            pltpu.VMEM(value.shape, value.dtype),
            pltpu.SMEM(middle_offsets.shape, jnp.int32),
            pltpu.SMEM(upper_offsets.shape, jnp.int32),
            pltpu.VMEM(out_weight.shape, out_weight.dtype),
            dma((6,)),
            pltpu.VMEM((pairs, taken, rows), jnp.bfloat16),
            pltpu.VMEM((pairs, 3 * HD, taken), jnp.bfloat16),
            pltpu.VMEM((seq_total, 3 * HD, taken), jnp.bfloat16),
            pltpu.VMEM((seq_total, HD + STAT_ROWS, taken), jnp.bfloat16),
            pltpu.VMEM((pairs, HD + STAT_ROWS, taken), jnp.bfloat16),
            pltpu.VMEM((heads, HD, rows), jnp.float32),
            pltpu.VMEM((heads, 8, rows), jnp.float32),
            pltpu.VMEM((4, width, taken), jnp.bfloat16),
            pltpu.VMEM((4, width, taken), jnp.bfloat16),
            pltpu.VMEM((4,) + out_weight.shape, jnp.bfloat16),
            dma((seq_total,)),
            dma((seq_total,)),
            dma((seq_total,)),
            dma((seq_total,)),
            dma((4,)),
            dma((4,)),
            dma((4,)),
            dma((4,)),
        ],
        compiler_params=pltpu.CompilerParams(
            collective_id=0, has_side_effects=True, vmem_limit_bytes=60 * 2**20
        ),
    )(query, key, value, middle_offsets, upper_offsets, out_weight)


def solution(mesh):
    in_specs = (
        P("seq", "head"),
        P("seq", "head"),
        P("seq", "head"),
        P("head"),
        P("head"),
        P("head", None),
    )
    out_specs = P(("seq", "head"), None)
    seq_total, head_shards = mesh.shape["seq"], mesh.shape["head"]
    one_segment = seq_total == SPAN and seq_total // 2 == MIDDLE_DILATION and head_shards == 4
    return jax.shard_map(
        per_device_fused if one_segment else per_device, mesh=mesh, in_specs=in_specs, out_specs=out_specs, check_vma=False
    )
```
